32 devices in a mesh: row: 4 (over x, core), col: 8 (over z, y).
Axes of the slice: x: 2, y: 2, z: 4, core: 2. Of those that a mesh axis runs over, the one named last changes fastest.
Arguments:
- amplitudes: bfloat16 [4, 1024, 1024], P(None, 'row', 'col'), may hold values from -6 to 6
- factors: bfloat16 [3072, 65536], P('col', 'row'), may hold values from -0.029907227 to 0.029907227
- tile_mask: int32 [16, 16], replicated, may hold values 0 or 1
- tile_irrep: int32 [16], replicated, may hold values from 0 to 1
Outputs:
- residual: float32 [4, 64, 64], P(None, 'row', 'col')
The draws below stay inside these ranges and needn't reach their ends.
All inputs are finite; a program needn't handle non-finite values.
Results may differ from the reference program's by a relative error of at most 0.007.
Values may be sent and summed in bfloat16 or wider, within the bound.
No kernel may reach another device: no remote copies, remote signals or barrier semaphores. Data moves between devices by JAX's collectives and lax.ppermute only.
A program may use at most 128 MiB of HBM per device.

```python
import jax
import jax.numpy as jnp
from jax import lax

NV = 1024
NT = 16
TILE = 64
NQ = 3072
NOCC = 2
NPAIR = 4
WIN = 64


def place_ends(drawn, stream_key, low, largest):
    index_at = [jax.random.randint(jax.random.fold_in(stream_key, axis), (), 0, length) for axis, length in enumerate(drawn.shape)]
    main_axis = drawn.shape.index(max(drawn.shape))
    beside = index_at[:main_axis] + [(index_at[main_axis] + 1) % drawn.shape[main_axis]] + index_at[main_axis + 1:]
    return drawn.at[tuple(index_at)].set(low).at[tuple(beside)].set(largest)


def spiked(entries, own_key, source, target, shards_of, factor):
    def block_of(dim):
        return (jnp.arange(entries.shape[dim]) // (entries.shape[dim] // shards_of)).reshape((-1,) + (1,) * (entries.ndim - 1 - dim))

    first = jax.random.permutation(own_key, shards_of)[block_of(target)]
    far = (block_of(target) + shards_of // 2) % shards_of
    return jnp.where((block_of(source) == first) | (block_of(source) == far), factor * entries, entries)


def steps_of(key, shape, shards, least, largest):
    def one(axis_at, parts):
        draws = jax.random.uniform(jax.random.fold_in(jax.random.fold_in(key, 6), axis_at), (parts,), jnp.float32, least / len(shards), largest / len(shards))
        return jnp.repeat(jnp.exp(draws), shape[axis_at] // parts).reshape((-1,) + (1,) * (len(shape) - axis_at - 1))

    gain = one(*shards[0])
    for cut in shards[1:]:
        gain = gain * one(*cut)
    return gain


def bell_draw(key, shape, spread, reach, cuts=(), kind=jnp.bfloat16):
    drawn = spread * jax.random.normal(key, shape, jnp.float32)
    if cuts:
        drawn = drawn * steps_of(key, shape, cuts, -0.22, 0.18)
    return jnp.clip(drawn, -reach, reach).astype(kind)


def bell_draw_with(rng, dims, spread, most, split, heavy, kind=jnp.bfloat16):
    entries = spread * jax.random.normal(rng, dims, jnp.float32)
    if split:
        entries = entries * steps_of(rng, dims, split, -0.22, 0.18)
    return jnp.clip(spiked(entries, jax.random.fold_in(rng, 3), *heavy), -most, most).astype(kind)


def setup_inputs(seed: int = 0) -> dict:
    arg_keys = jax.random.split(jax.random.key(seed), 5)
    amplitudes = bell_draw(arg_keys[0], (NPAIR, NV, NV), 1.0, 6.0, ((1, 4), (2, 8)))
    factors = bell_draw_with(arg_keys[1], (NQ, NV * WIN), 0.005, 0.029907227, ((0, 8), (1, 4)), (0, 1, 8, 2.0))
    tile_mask = place_ends((jax.random.randint(arg_keys[2], (NT, NT), 0, 8) < 7).astype(jnp.int32), jax.random.fold_in(arg_keys[2], 1), 0, 1)
    tile_irrep = place_ends(jax.random.randint(arg_keys[3], (NT,), 0, 2), jax.random.fold_in(arg_keys[3], 1), 0, 1).astype(jnp.int32)
    return {"amplitudes": amplitudes, "factors": factors, "tile_mask": tile_mask, "tile_irrep": tile_irrep}


def reference(amplitudes, factors, tile_mask, tile_irrep):
    pair_index = jnp.arange(NPAIR, dtype=jnp.int32)
    first_occ = pair_index // NOCC
    second_occ = pair_index % NOCC
    pair_irrep = jnp.bitwise_xor(first_occ % 2, second_occ % 2).astype(jnp.int32)
    cross_irrep = jnp.bitwise_xor(tile_irrep[:, None], tile_irrep[None, :])
    live_tiles = tile_mask[None, :, :] * (cross_irrep[None, :, :] == pair_irrep[:, None, None]).astype(jnp.int32)
    shaped = amplitudes.reshape(NPAIR, NT, TILE, NT, TILE)
    masked = (shaped * live_tiles.astype(jnp.bfloat16)[:, :, None, :, None]).reshape(NPAIR, NT, TILE, NV)
    masked_wide = masked.astype(jnp.float32)
    q_block = 8

    def add_block(running, fac_block):
        near_side = fac_block.reshape(q_block, NT, TILE, WIN).astype(jnp.float32)
        partial_value = jnp.einsum('qkca,pkcd->qpkad', near_side, masked_wide)
        rounded = lax.optimization_barrier(partial_value.astype(jnp.bfloat16)).astype(jnp.float32)
        running = running + jnp.einsum('qpkad,qdb->pab', rounded, fac_block.astype(jnp.float32))
        return running, None

    start_sum = jnp.zeros((NPAIR, WIN, WIN), jnp.float32)
    ladder, _ = lax.scan(add_block, start_sum, factors.reshape(NQ // q_block, q_block, NV, WIN))
    mirror_term = ladder.reshape(NOCC, NOCC, WIN, WIN).transpose(1, 0, 3, 2).reshape(NPAIR, WIN, WIN)
    return ladder + mirror_term
```

```python
import functools

import jax
import jax.numpy as jnp
from jax import lax
from jax.experimental import pallas as pl
from jax.experimental.pallas import tpu as pltpu
from jax.sharding import PartitionSpec as P

TILE = 64
NOCC = 2
WIN = 64
LANES = 2 * WIN
BLOCK = 256


def chunk_sizes(total):
    if total >= 64 and total % 16 == 0:
        sizes = [16] * (total // 16 - 1) + [8, 8]
        return sizes
    return [total]


def group_of(count):
    for size in (8, 4, 2):
        if count % size == 0:
            return size
    return 1


def deinterleave(length):
    half = length // 2
    source = jnp.arange(length, dtype=jnp.int32)
    target = source % 2 * half + source // 2
    return (target[:, None] == jnp.arange(length, dtype=jnp.int32)[None, :]).astype(jnp.bfloat16)


def ladder_kernel(b_ref, t_ref, acc_ref, o_ref, lhs, xs, *, group, pair_count, d_half):
    half = b_ref.shape[0] * b_ref.shape[2]
    width = 2 * half

    @pl.when(pl.program_id(0) == 0)
    def _():
        o_ref[...] = acc_ref[...]

    for q in range(group):
        b_q = b_ref[:, q].reshape(half, LANES)
        for j in range(half // LANES):
            turned = b_q[j * LANES : (j + 1) * LANES].T
            rows = slice(q * WIN, (q + 1) * WIN)
            lhs[rows, 2 * j * LANES : (2 * j + 1) * LANES] = turned[:WIN]
            lhs[rows, (2 * j + 1) * LANES : (2 * j + 2) * LANES] = turned[WIN:]
    low = lax.broadcasted_iota(jnp.int32, (d_half, LANES), 1) < WIN
    for block in range(width // BLOCK):
        for p in range(pair_count):
            x = jnp.dot(
                lhs[...], t_ref[p, :, block * BLOCK : (block + 1) * BLOCK], preferred_element_type=jnp.float32
            ).astype(jnp.bfloat16)
            for q in range(group):
                xs[q, p * WIN : (p + 1) * WIN, :] = x[q * WIN : (q + 1) * WIN]
        for q in range(group):
            b_q = b_ref[:, q].reshape(half, LANES)
            pieces = []
            for i in range(BLOCK // (2 * d_half)):
                start = block * (BLOCK // 2) + i * d_half
                piece = b_q[start : start + d_half]
                zero = jnp.zeros_like(piece)
                pieces += [jnp.where(low, piece, zero), jnp.where(low, zero, piece)]
            o_ref[...] += jnp.dot(xs[q], jnp.concatenate(pieces, 0), preferred_element_type=jnp.float32)


def contract(acc, b_chunk, planes, d_half):
    rows, count, height, _ = b_chunk.shape
    pair_count, width, _ = planes.shape
    group = group_of(count)
    return pl.pallas_call(
        functools.partial(ladder_kernel, group=group, pair_count=pair_count, d_half=d_half),
        grid=(count // group,),
        in_specs=[
            pl.BlockSpec((rows, group, height, LANES), lambda i: (0, i, 0, 0)),
            pl.BlockSpec((pair_count, width, width), lambda i: (0, 0, 0), pipeline_mode=pl.Buffered(1)),
            pl.BlockSpec(acc.shape, lambda i: (0, 0)),
        ],
        out_specs=pl.BlockSpec(acc.shape, lambda i: (0, 0)),
        out_shape=jax.ShapeDtypeStruct(acc.shape, jnp.float32),
        scratch_shapes=[
            pltpu.VMEM((group * WIN, width), jnp.bfloat16),
            pltpu.VMEM((group, pair_count * WIN, BLOCK), jnp.bfloat16),
        ],
        compiler_params=pltpu.CompilerParams(vmem_limit_bytes=40 << 20),
        cost_estimate=pl.CostEstimate(
            flops=2 * count * pair_count * WIN * width * (width + LANES),
            bytes_accessed=2 * count * width * WIN + 2 * planes.size,
            transcendentals=0,
        ),
    )(b_chunk, planes, acc)


def ring_gather(piece, axis, order):
    size = len(order)
    place = [order.index(k) for k in range(size)]
    me = jnp.asarray(place, jnp.int32)[lax.axis_index(axis)]
    table = jnp.asarray(order, jnp.int32)
    ahead = [(order[i], order[(i + 1) % size]) for i in range(size)]
    behind = [(b, a) for a, b in ahead]
    height, width = piece.shape
    half = height // 2
    whole = jnp.zeros((height, size * width), piece.dtype)

    def put(whole, part, top, step):
        return lax.dynamic_update_slice(whole, part, (top, table[(me + step) % size] * width))

    up, down = piece[:half], piece[half:]
    whole = put(whole, piece, 0, 0)
    for step in range(1, size):
        up = lax.ppermute(up, axis, ahead)
        down = lax.ppermute(down, axis, behind)
        whole = put(whole, up, 0, size - step)
        whole = put(whole, down, half, step)
    return whole


def amplitude_planes(amplitudes, tile_mask, tile_irrep, row_count, col_count):
    pair_count, c_here, d_here = amplitudes.shape
    tile_count = tile_mask.shape[0]
    c_all, d_all = c_here * row_count, d_here * col_count
    row, col = lax.axis_index("row"), lax.axis_index("col")
    c_tiles, d_tiles = c_here // TILE, d_here // TILE
    here = lax.dynamic_slice(tile_mask, (row * c_tiles, col * d_tiles), (c_tiles, d_tiles))
    c_irrep = lax.dynamic_slice_in_dim(tile_irrep, row * c_tiles, c_tiles)
    d_irrep = lax.dynamic_slice_in_dim(tile_irrep, col * d_tiles, d_tiles)
    cross = jnp.bitwise_xor(c_irrep[:, None], d_irrep[None, :])

    def spread(small):
        return jnp.repeat(jnp.repeat(small, TILE, 0), TILE, 1)

    keep, same = spread(here) != 0, spread(cross) == 0
    zero = jnp.zeros((), amplitudes.dtype)
    plane_a = jnp.where(keep, jnp.where(same, amplitudes[0], amplitudes[1]), zero)
    plane_b = jnp.where(keep, jnp.where(same, amplitudes[3], amplitudes[2]), zero)
    to_send = jnp.stack([plane_a, plane_b] * (row_count // 2))
    mine = lax.all_to_all(to_send, "row", 0, 0)
    blocked = mine.reshape(c_all // BLOCK, BLOCK, d_here)
    turned = jnp.einsum(
        "cx,jcd->jxd", deinterleave(BLOCK), blocked, preferred_element_type=jnp.float32
    ).astype(jnp.bfloat16)
    turned = jnp.einsum(
        "jxd,dy->jxy", turned, deinterleave(d_here), preferred_element_type=jnp.float32
    ).astype(jnp.bfloat16)
    order = list(range(0, col_count, 2)) + list(range(1, col_count, 2))[::-1]
    whole = ring_gather(turned.reshape(c_all, d_here), "col", order)
    other = lax.ppermute(whole, "row", [(i, i ^ 1) for i in range(row_count)])
    even = row % 2 == 0
    planes = jnp.stack([jnp.where(even, whole, other), jnp.where(even, other, whole)])
    c_order = jnp.broadcast_to(
        tile_irrep.reshape(-1, 1, BLOCK // TILE, 1), (c_all // BLOCK, 2, BLOCK // TILE, TILE // 2)
    ).reshape(c_all)
    d_order = jnp.broadcast_to(
        tile_irrep.reshape(-1, 1, d_tiles, 1), (col_count, 2, d_tiles, TILE // 2)
    ).reshape(d_all)
    cross_all = jnp.bitwise_xor(c_order[:, None], d_order[None, :])
    return jnp.stack(
        [
            jnp.where(cross_all == 0, planes[0], zero),
            jnp.where(cross_all == 1, planes[0], zero),
            jnp.where(cross_all == 1, planes[1], zero),
            jnp.where(cross_all == 0, planes[1], zero),
        ]
    )


def per_device(amplitudes, factors, tile_mask, tile_irrep, *, row_count, col_count):
    pair_count = amplitudes.shape[0]
    d_half = amplitudes.shape[2] // 2
    planes = amplitude_planes(amplitudes, tile_mask, tile_irrep, row_count, col_count)
    q_here, flat = factors.shape
    height = flat // LANES
    acc = jnp.zeros((pair_count * WIN, LANES), jnp.float32)
    start = 0
    chunks = []
    for count in chunk_sizes(q_here // row_count):
        piece = factors[start * row_count : (start + count) * row_count].reshape(row_count, count, height, LANES)
        chunks.append(lax.all_to_all(piece, "row", 0, 0))
        start += count
    for chunk in chunks:
        acc = contract(acc, chunk, planes, d_half)
    ladder = (acc[:, :WIN] + acc[:, WIN:]).reshape(NOCC, NOCC, WIN, WIN)
    flipped = ladder.transpose(1, 0, 2, 3) + ladder.transpose(0, 1, 3, 2)
    a_count, b_count = WIN // row_count, WIN // col_count
    blocks = flipped.reshape(pair_count, col_count, b_count, row_count, a_count).transpose(3, 1, 0, 2, 4)
    blocks = blocks.reshape(row_count * col_count, pair_count * b_count * a_count)
    summed = lax.all_to_all(blocks, ("row", "col"), 0, 0, tiled=True).sum(0)
    return summed.reshape(pair_count, b_count, a_count).transpose(0, 2, 1)


def solution(mesh):
    return jax.shard_map(
        functools.partial(per_device, row_count=mesh.shape["row"], col_count=mesh.shape["col"]),
        mesh=mesh,
        in_specs=(P(None, "row", "col"), P("col", "row"), P(), P()),
        out_specs=P(None, "row", "col"),
        check_vma=False,
    )
```

```python
import functools

import jax
import jax.numpy as jnp
from jax import lax
from jax.experimental import pallas as pl
from jax.experimental.pallas import tpu as pltpu
from jax.sharding import PartitionSpec as P

TILE = 64
WIN = 64
LANES = 2 * WIN
BLOCK = 256


def chunk_sizes(total):
    middle = (total - 32) // 2
    if middle >= 16 and total % 16 == 0:
        return [8, middle, middle, 16, 8]
    return [total]


def group_of(count):
    for size in (8, 4, 2):
        if count % size == 0:
            return size
    return 1


def deinterleave(length, transposed=False):
    half = length // 2
    source = lax.broadcasted_iota(jnp.int32, (length, length), 1 if transposed else 0)
    target = lax.broadcasted_iota(jnp.int32, (length, length), 0 if transposed else 1)
    return (source % 2 * half + source // 2 == target).astype(jnp.float32).astype(jnp.bfloat16)


def relative(values, row):
    count = values.shape[0]
    bit = 1
    while bit < count:
        pairs = values.reshape((count // (2 * bit), 2, bit) + values.shape[1:])
        values = jnp.where(row & bit != 0, pairs[:, ::-1], pairs).reshape(values.shape)
        bit *= 2
    return values


def split_kernel(row_ref, *refs):
    half = len(refs) // 2
    for source, target in zip(refs[:half], refs[half:]):
        target[...] = source[...].reshape(target.shape)


def split_chunk(factors, row, start, count, row_count):
    flat = factors.shape[1]
    height = flat // LANES
    step = 8
    if count % step:
        return [
            lax.dynamic_slice_in_dim(factors, start * row_count + (row ^ x) * count, count, 0).reshape(
                count, height, LANES
            )
            for x in range(row_count)
        ]
    base = start * row_count // step

    def source_map(x, i, row_ref):
        return base + (row_ref[0] ^ x) * (count // step) + i, 0

    return pl.pallas_call(
        split_kernel,
        grid_spec=pltpu.PrefetchScalarGridSpec(
            num_scalar_prefetch=1,
            grid=(count // step,),
            in_specs=[pl.BlockSpec((step, flat), functools.partial(source_map, x)) for x in range(row_count)],
            out_specs=[pl.BlockSpec((step, height, LANES), lambda i, row_ref: (i, 0, 0))] * row_count,
        ),
        out_shape=[jax.ShapeDtypeStruct((count, height, LANES), factors.dtype)] * row_count,
        compiler_params=pltpu.CompilerParams(vmem_limit_bytes=16 << 20),
        cost_estimate=pl.CostEstimate(
            flops=0, bytes_accessed=4 * count * row_count * flat, transcendentals=0
        ),
    )(row[None], *([pltpu.with_memory_space_constraint(factors, pltpu.HBM)] * row_count))


def ladder_kernel(*refs, rows, group, plane_count):
    b_refs, (t_ref, acc_ref, o_ref, lhs, xs) = refs[:rows], refs[rows:]
    half = rows * b_refs[0].shape[1]

    @pl.when(pl.program_id(0) == 0)
    def _():
        o_ref[...] = acc_ref[...]

    def rows_of(q):
        return jnp.concatenate([b_ref[q] for b_ref in b_refs], 0)

    for q in range(group):
        b_q = rows_of(q)
        for j in range(half // LANES):
            turned = b_q[j * LANES : (j + 1) * LANES].T
            here = slice(q * WIN, (q + 1) * WIN)
            lhs[here, 2 * j * LANES : (2 * j + 1) * LANES] = turned[:WIN]
            lhs[here, (2 * j + 1) * LANES : (2 * j + 2) * LANES] = turned[WIN:]
    low = lax.broadcasted_iota(jnp.int32, (LANES, LANES), 1) < WIN
    for block in range(half // LANES):
        columns = slice(block * BLOCK, (block + 1) * BLOCK)
        for plane in range(plane_count):
            depth = 2 * half if plane == plane_count - 1 else (block + 1) * BLOCK
            x = jnp.dot(
                lhs[:, :depth], t_ref[plane, :depth, columns], preferred_element_type=jnp.float32
            ).astype(jnp.bfloat16)
            for q in range(group):
                xs[q, plane * WIN : (plane + 1) * WIN, :] = x[q * WIN : (q + 1) * WIN]
        for q in range(group):
            piece = rows_of(q)[block * LANES : (block + 1) * LANES]
            zero = jnp.zeros_like(piece)
            both = jnp.concatenate([jnp.where(low, piece, zero), jnp.where(low, zero, piece)], 0)
            o_ref[...] += jnp.dot(xs[q], both, preferred_element_type=jnp.float32)


def contract(acc, pieces, planes):
    rows = len(pieces)
    count, height, _ = pieces[0].shape
    plane_count, width, _ = planes.shape
    group = group_of(count)
    return pl.pallas_call(
        functools.partial(ladder_kernel, rows=rows, group=group, plane_count=plane_count),
        grid=(count // group,),
        in_specs=[pl.BlockSpec((group, height, LANES), lambda i: (i, 0, 0))] * rows
        + [pl.BlockSpec(memory_space=pltpu.VMEM)]
        + [pl.BlockSpec(acc.shape, lambda i: (0, 0))],
        out_specs=pl.BlockSpec(acc.shape, lambda i: (0, 0)),
        out_shape=jax.ShapeDtypeStruct(acc.shape, jnp.float32),
        scratch_shapes=[
            pltpu.VMEM((group * WIN, width), jnp.bfloat16),
            pltpu.VMEM((group, plane_count * WIN, BLOCK), jnp.bfloat16),
        ],
        compiler_params=pltpu.CompilerParams(vmem_limit_bytes=24 << 20),
        cost_estimate=pl.CostEstimate(
            flops=2 * count * plane_count * WIN * width * width,
            bytes_accessed=2 * count * width * WIN,
            transcendentals=0,
        ),
    )(*pieces, planes, acc)


def ring_gather(piece, axis, size):
    order = list(range(0, size, 2)) + list(range(1, size, 2))[::-1]
    ahead = [(order[i], order[(i + 1) % size]) for i in range(size)]
    behind = [(b, a) for a, b in ahead]
    me = lax.axis_index(axis)
    place = jnp.where(me % 2 == 0, me // 2, size - 1 - me // 2)
    height, width = piece.shape
    half = height // 2
    whole = jnp.zeros((height, size * width), piece.dtype)

    def put(whole, part, top, step):
        at = (place + step) % size
        owner = jnp.where(2 * at < size, 2 * at, 2 * size - 1 - 2 * at)
        return lax.dynamic_update_slice(whole, part, (top, owner * width))

    up, down = piece[:half], piece[half:]
    whole = put(whole, piece, 0, 0)
    for step in range(1, size):
        up = lax.ppermute(up, axis, ahead)
        down = lax.ppermute(down, axis, behind)
        whole = put(whole, up, 0, size - step)
        whole = put(whole, down, half, step)
    return whole


def pack_kernel(at_ref, mask_ref, irrep_ref, t_ref, o_ref, *, turned):
    _, c_here, d_here = t_ref.shape
    c_tiles, d_tiles = c_here // TILE, d_here // TILE
    lane_tile = lax.broadcasted_iota(jnp.int32, (TILE, d_here), 1) // TILE
    planes = [[], []]
    for ct in range(c_tiles):
        c_tile = at_ref[0] * c_tiles + ct
        keep = jnp.zeros((TILE, d_here), jnp.int32)
        cross = jnp.zeros((TILE, d_here), jnp.int32)
        for dt in range(d_tiles):
            d_tile = at_ref[1] * d_tiles + dt
            keep = jnp.where(lane_tile == dt, mask_ref[c_tile, d_tile], keep)
            cross = jnp.where(lane_tile == dt, irrep_ref[c_tile] ^ irrep_ref[d_tile], cross)
        t = [t_ref[p, ct * TILE : (ct + 1) * TILE].astype(jnp.float32) for p in range(4)]
        for plane, (first, second) in zip(planes, ((t[0], t[1]), (t[3], t[2]))):
            chosen = jnp.where(cross == 0, first, second)
            plane.append(jnp.where(keep != 0, chosen, 0.0).astype(jnp.bfloat16))
    for s, plane in enumerate(planes):
        value = jnp.concatenate(plane, 0)
        if turned:
            value = jnp.dot(deinterleave(BLOCK, True), value, preferred_element_type=jnp.float32).astype(jnp.bfloat16)
            value = jnp.dot(value, deinterleave(d_here), preferred_element_type=jnp.float32).astype(jnp.bfloat16)
        for r in range(s, o_ref.shape[0], 2):
            o_ref[r] = value


def fits(c_here, d_here):
    return c_here == BLOCK and d_here == LANES


def pack(amplitudes, tile_mask, tile_irrep, row, col, row_count):
    _, c_here, d_here = amplitudes.shape
    return pl.pallas_call(
        functools.partial(pack_kernel, turned=fits(c_here, d_here)),
        in_specs=[pl.BlockSpec(memory_space=pltpu.SMEM)] * 3 + [pl.BlockSpec(memory_space=pltpu.VMEM)],
        out_specs=pl.BlockSpec(memory_space=pltpu.VMEM),
        out_shape=jax.ShapeDtypeStruct((row_count, c_here, d_here), jnp.bfloat16),
        compiler_params=pltpu.CompilerParams(vmem_limit_bytes=8 << 20),
        cost_estimate=pl.CostEstimate(flops=1 << 24, bytes_accessed=amplitudes.size * 2, transcendentals=0),
    )(jnp.stack([row, col]), tile_mask, tile_irrep, amplitudes)


def expand_kernel(row_ref, irrep_ref, own_ref, other_ref, o_ref):
    row = row_ref[0]
    count = own_ref.shape[0] // BLOCK
    tiles = BLOCK // TILE
    even = row % 2 == 0
    low = lax.broadcasted_iota(jnp.int32, (BLOCK, LANES), 1) < WIN

    def at(block):
        return pl.ds(pl.multiple_of(block * BLOCK, BLOCK), BLOCK)

    def planes(i, j):
        def ordered(ref):
            value = ref[at(i ^ row), at(j ^ row)].astype(jnp.float32)
            first, second = value[:, :LANES], value[:, LANES:]
            return jnp.concatenate(
                [
                    jnp.where(low, first, pltpu.roll(second, WIN, 1)),
                    jnp.where(low, pltpu.roll(first, WIN, 1), second),
                ],
                1,
            )

        own, other = ordered(own_ref), ordered(other_ref)
        return jnp.where(even, own, other), jnp.where(even, other, own)

    def irreps(block, axis):
        tile = lax.broadcasted_iota(jnp.int32, (BLOCK, BLOCK), axis) % LANES // (TILE // 2)
        value = jnp.zeros((BLOCK, BLOCK), jnp.int32)
        for t in range(tiles):
            value = jnp.where(tile == t, irrep_ref[(block ^ row) * tiles + t], value)
        return value

    def put(plane, i, j, value):
        o_ref[plane, at(i), at(j)] = value.astype(jnp.bfloat16)

    @pl.loop(0, count)
    def _(i):
        same = irreps(i, 0) == irreps(i, 1)
        a, b = planes(i, i)
        put(0, i, i, jnp.where(same, a, 0.0))
        put(1, i, i, jnp.where(same, b, 0.0))
        put(2, i, i, jnp.where(same, 0.0, a + b.T))

        @pl.loop(i + 1, count)
        def _(j):
            same = irreps(i, 0) == irreps(j, 1)
            a_up, b_up = planes(i, j)
            a_down, b_down = planes(j, i)
            b_turned = b_down.T
            put(0, i, j, jnp.where(same, a_up + a_down.T, 0.0))
            put(1, i, j, jnp.where(same, b_up + b_turned, 0.0))
            put(2, i, j, jnp.where(same, 0.0, a_up + b_turned))
            same = irreps(j, 0) == irreps(i, 1)
            put(2, j, i, jnp.where(same, 0.0, a_down + b_up.T))


def expand(own, other, tile_irrep, row):
    vmem = pl.BlockSpec(memory_space=pltpu.VMEM)
    return pl.pallas_call(
        expand_kernel,
        in_specs=[pl.BlockSpec(memory_space=pltpu.SMEM)] * 2 + [vmem] * 2,
        out_specs=vmem,
        out_shape=jax.ShapeDtypeStruct((3, *own.shape), own.dtype),
        compiler_params=pltpu.CompilerParams(vmem_limit_bytes=12 << 20),
        cost_estimate=pl.CostEstimate(flops=1 << 24, bytes_accessed=own.size * 10, transcendentals=0),
    )(row[None], tile_irrep, own, other)


def expand_small(own, other, tile_irrep, row, row_count):
    size = own.shape[0]
    c_here = size // row_count
    even = row % 2 == 0

    def by_row(plane):
        moved = relative(plane.reshape(row_count, c_here, size), row).reshape(size // BLOCK, BLOCK, size)
        return jnp.einsum(
            "xc,jcd->jxd", deinterleave(BLOCK, True), moved, preferred_element_type=jnp.float32
        ).reshape(size, size)

    def ordered(plane):
        return by_row(by_row(plane).astype(plane.dtype).T).T

    own, other = ordered(own), ordered(other)
    a, b = jnp.where(even, own, other), jnp.where(even, other, own)
    irrep = relative(tile_irrep.reshape(row_count, c_here // TILE), row)
    order = jnp.broadcast_to(
        irrep.reshape(-1, 1, BLOCK // TILE, 1), (size // BLOCK, 2, BLOCK // TILE, TILE // 2)
    ).reshape(size)
    same = order[:, None] == order[None, :]
    block = jnp.arange(size, dtype=jnp.int32) // BLOCK
    above, level = block[:, None] < block[None, :], block[:, None] == block[None, :]

    def upper(plane):
        chosen = jnp.where(level, plane, jnp.where(above, plane + plane.T, 0.0))
        return jnp.where(same, chosen, 0.0)

    return jnp.stack([upper(a), upper(b), jnp.where(same, 0.0, a + b.T)]).astype(jnp.bfloat16)


def amplitude_planes(amplitudes, tile_mask, tile_irrep, row, col, row_count, col_count):
    _, c_here, d_here = amplitudes.shape
    to_send = pack(amplitudes, tile_mask, tile_irrep, row, col, row_count)
    mine = lax.all_to_all(to_send, "row", 0, 0)
    own = ring_gather(mine.reshape(c_here * row_count, d_here), "col", col_count)
    other = lax.ppermute(own, "row", [(i, i ^ 1) for i in range(row_count)])
    if fits(c_here, d_here):
        return expand(own, other, tile_irrep, row)
    return expand_small(own, other, tile_irrep, row, row_count)


def per_device(amplitudes, factors, tile_mask, tile_irrep, *, row_count, col_count):
    pair_count = amplitudes.shape[0]
    row, col = lax.axis_index("row"), lax.axis_index("col")
    acc = jnp.zeros((3 * WIN, LANES), jnp.float32)
    chunks = []
    start = 0
    for count in chunk_sizes(factors.shape[0] // row_count):
        pieces = split_chunk(factors, row, start, count, row_count)
        arrived = [pieces[0]]
        for x in range(1, row_count):
            arrived.append(lax.ppermute(pieces[x], "row", [(i, i ^ x) for i in range(row_count)]))
        chunks.append(arrived)
        start += count
    planes = amplitude_planes(amplitudes, tile_mask, tile_irrep, row, col, row_count, col_count)
    for chunk in chunks:
        acc = contract(acc, chunk, planes)
    upper = (acc[:, :WIN] + acc[:, WIN:]).reshape(3, WIN, WIN)
    turned = upper.transpose(0, 2, 1)
    flipped = jnp.stack([upper[0] + turned[0], turned[2], upper[2], upper[1] + turned[1]])
    a_count, b_count = WIN // row_count, WIN // col_count
    blocks = flipped.reshape(pair_count, col_count, b_count, row_count, a_count).transpose(3, 1, 0, 2, 4)
    blocks = blocks.reshape(row_count * col_count, pair_count * b_count * a_count)
    summed = lax.all_to_all(blocks, ("row", "col"), 0, 0, tiled=True).sum(0)
    return summed.reshape(pair_count, b_count, a_count).transpose(0, 2, 1)


def solution(mesh):
    row_count, col_count = mesh.shape["row"], mesh.shape["col"]
    return jax.shard_map(
        functools.partial(per_device, row_count=row_count, col_count=col_count),
        mesh=mesh,
        in_specs=(P(None, "row", "col"), P("col", "row"), P(), P()),
        out_specs=P(None, "row", "col"),
        check_vma=False,
    )
```

```python
import functools

import jax
import jax.numpy as jnp
from jax import lax
from jax.experimental import pallas as pl
from jax.experimental.pallas import tpu as pltpu
from jax.sharding import PartitionSpec as P

TILE = 64
WIN = 64
LANES = 2 * WIN
BLOCK = 256


def chunk_sizes(total):
    middle = (total - 32) // 2
    if middle >= 16 and total % 16 == 0:
        return [8, middle, middle, 16, 8]
    return [total]


def group_of(count):
    for size in (8, 4, 2):
        if count % size == 0:
            return size
    return 1


def deinterleave(length, transposed=False):
    half = length // 2
    source = lax.broadcasted_iota(jnp.int32, (length, length), 1 if transposed else 0)
    target = lax.broadcasted_iota(jnp.int32, (length, length), 0 if transposed else 1)
    return (source % 2 * half + source // 2 == target).astype(jnp.float32).astype(jnp.bfloat16)


def relative(values, row):
    count = values.shape[0]
    bit = 1
    while bit < count:
        pairs = values.reshape((count // (2 * bit), 2, bit) + values.shape[1:])
        values = jnp.where(row & bit != 0, pairs[:, ::-1], pairs).reshape(values.shape)
        bit *= 2
    return values


def split_kernel(row_ref, *refs):
    half = len(refs) // 2
    step = refs[0].shape[0]
    here = pl.ds(pl.program_id(0) * step, step)
    for source, target in zip(refs[:half], refs[half:]):
        target[here] = source[...].reshape(step, *target.shape[1:])


def split_chunk(factors, row, start, count, row_count, steps):
    flat = factors.shape[1]
    height = flat // LANES
    step = 8
    if count % step:
        return [
            lax.dynamic_slice_in_dim(factors, start * row_count + (row ^ x) * count, count, 0).reshape(
                count, height, LANES
            )
            for x in steps
        ]
    base = start * row_count // step

    def source_map(x, i, row_ref):
        return base + (row_ref[0] ^ x) * (count // step) + i, 0

    return pl.pallas_call(
        split_kernel,
        grid_spec=pltpu.PrefetchScalarGridSpec(
            num_scalar_prefetch=1,
            grid=(count // step,),
            in_specs=[pl.BlockSpec((step, flat), functools.partial(source_map, x)) for x in steps],
            out_specs=[pl.BlockSpec(memory_space=pltpu.VMEM)] * len(steps),
        ),
        out_shape=[jax.ShapeDtypeStruct((count, height, LANES), factors.dtype)] * len(steps),
        compiler_params=pltpu.CompilerParams(vmem_limit_bytes=8 << 20),
        cost_estimate=pl.CostEstimate(
            flops=0, bytes_accessed=4 * count * len(steps) * flat, transcendentals=0
        ),
    )(row[None], *([pltpu.with_memory_space_constraint(factors, pltpu.HBM)] * len(steps)))


def ladder_kernel(*refs, rows, group, team, plane_count):
    b_refs, (t_ref, acc_ref, o_ref, lhs, xs, rhs) = refs[:rows], refs[rows:]
    half = rows * b_refs[0].shape[1]
    tall = plane_count * WIN
    low = lax.broadcasted_iota(jnp.int32, (tall, LANES), 1) < WIN
    o_ref[...] = acc_ref[...]

    @pl.loop(0, b_refs[0].shape[0] // group)
    def _(step):
        b_all = [jnp.concatenate([b_ref[step * group + q] for b_ref in b_refs], 0) for q in range(group)]
        for q, b_q in enumerate(b_all):
            for j in range(half // LANES):
                turned = b_q[j * LANES : (j + 1) * LANES].T
                here = slice(q * WIN, (q + 1) * WIN)
                lhs[here, 2 * j * LANES : (2 * j + 1) * LANES] = turned[:WIN]
                lhs[here, (2 * j + 1) * LANES : (2 * j + 2) * LANES] = turned[WIN:]
        for block in range(half // LANES):
            columns = slice(block * BLOCK, (block + 1) * BLOCK)
            for plane in range(plane_count):
                depth = 2 * half if plane == plane_count - 1 else (block + 1) * BLOCK
                x = jnp.dot(
                    lhs[:, :depth], t_ref[plane, :depth, columns], preferred_element_type=jnp.float32
                ).astype(jnp.bfloat16)
                for q in range(group):
                    top = q % team * tall + plane * WIN
                    xs[q // team, top : top + WIN, columns] = x[q * WIN : (q + 1) * WIN]
        for q in range(0, group, 2):
            lanes = slice(q % team * WIN, (q % team + 2) * WIN)
            for j in range(half // LANES):
                first, second = (b_all[q + k][j * LANES : (j + 1) * LANES] for k in range(2))
                rhs[q // team, 2 * j * LANES : (2 * j + 1) * LANES, lanes] = jnp.concatenate(
                    [first[:, :WIN], second[:, :WIN]], 1
                )
                rhs[q // team, (2 * j + 1) * LANES : (2 * j + 2) * LANES, lanes] = jnp.concatenate(
                    [first[:, WIN:], second[:, WIN:]], 1
                )
        for t in range(group // team):
            y = jnp.dot(xs[t], rhs[t], preferred_element_type=jnp.float32)
            for q in range(0, team, 2):
                lanes = slice(q * WIN, (q + 2) * WIN)
                o_ref[...] += jnp.where(low, y[q * tall : (q + 1) * tall, lanes], y[(q + 1) * tall : (q + 2) * tall, lanes])


def contract(acc, pieces, planes):
    rows = len(pieces)
    count = pieces[0].shape[0]
    plane_count, width, _ = planes.shape
    group = group_of(count)
    team = min(group, 4)
    vmem = pl.BlockSpec(memory_space=pltpu.VMEM)
    return pl.pallas_call(
        functools.partial(ladder_kernel, rows=rows, group=group, team=team, plane_count=plane_count),
        in_specs=[vmem] * (rows + 2),
        out_specs=vmem,
        out_shape=jax.ShapeDtypeStruct(acc.shape, jnp.float32),
        scratch_shapes=[
            pltpu.VMEM((group * WIN, width), jnp.bfloat16),
            pltpu.VMEM((group // team, team * plane_count * WIN, width), jnp.bfloat16),
            pltpu.VMEM((group // team, width, team * WIN), jnp.bfloat16),
        ],
        compiler_params=pltpu.CompilerParams(vmem_limit_bytes=10 << 20),
        cost_estimate=pl.CostEstimate(
            flops=2 * count * plane_count * WIN * width * width,
            bytes_accessed=2 * count * width * WIN,
            transcendentals=0,
        ),
    )(*pieces, planes, acc)


def ring_gather(piece, axis, size):
    order = list(range(0, size, 2)) + list(range(1, size, 2))[::-1]
    ahead = [(order[i], order[(i + 1) % size]) for i in range(size)]
    behind = [(b, a) for a, b in ahead]
    me = lax.axis_index(axis)
    place = jnp.where(me % 2 == 0, me // 2, size - 1 - me // 2)
    height, width = piece.shape
    half = height // 2
    whole = jnp.zeros((height, size * width), piece.dtype)

    def put(whole, part, top, step):
        at = (place + step) % size
        owner = jnp.where(2 * at < size, 2 * at, 2 * size - 1 - 2 * at)
        return lax.dynamic_update_slice(whole, part, (top, owner * width))

    up, down = piece[:half], piece[half:]
    whole = put(whole, piece, 0, 0)
    for step in range(1, size):
        up = lax.ppermute(up, axis, ahead)
        down = lax.ppermute(down, axis, behind)
        whole = put(whole, up, 0, size - step)
        whole = put(whole, down, half, step)
    return whole


def pack_kernel(at_ref, mask_ref, irrep_ref, t_ref, o_ref, *, turned):
    _, c_here, d_here = t_ref.shape
    c_tiles, d_tiles = c_here // TILE, d_here // TILE
    lane_tile = lax.broadcasted_iota(jnp.int32, (TILE, d_here), 1) // TILE
    planes = [[], []]
    for ct in range(c_tiles):
        c_tile = at_ref[0] * c_tiles + ct
        keep = jnp.zeros((TILE, d_here), jnp.int32)
        cross = jnp.zeros((TILE, d_here), jnp.int32)
        for dt in range(d_tiles):
            d_tile = at_ref[1] * d_tiles + dt
            keep = jnp.where(lane_tile == dt, mask_ref[c_tile, d_tile], keep)
            cross = jnp.where(lane_tile == dt, irrep_ref[c_tile] ^ irrep_ref[d_tile], cross)
        t = [t_ref[p, ct * TILE : (ct + 1) * TILE].astype(jnp.float32) for p in range(4)]
        for plane, (first, second) in zip(planes, ((t[0], t[1]), (t[3], t[2]))):
            chosen = jnp.where(cross == 0, first, second)
            plane.append(jnp.where(keep != 0, chosen, 0.0).astype(jnp.bfloat16))
    for s, plane in enumerate(planes):
        value = jnp.concatenate(plane, 0)
        if turned:
            value = jnp.dot(deinterleave(BLOCK, True), value, preferred_element_type=jnp.float32).astype(jnp.bfloat16)
            value = jnp.dot(value, deinterleave(d_here), preferred_element_type=jnp.float32).astype(jnp.bfloat16)
        for r in range(s, o_ref.shape[0], 2):
            o_ref[r] = value


def fits(c_here, d_here):
    return c_here == BLOCK and d_here == LANES


def pack(amplitudes, tile_mask, tile_irrep, row, col, row_count):
    _, c_here, d_here = amplitudes.shape
    return pl.pallas_call(
        functools.partial(pack_kernel, turned=fits(c_here, d_here)),
        in_specs=[pl.BlockSpec(memory_space=pltpu.SMEM)] * 3 + [pl.BlockSpec(memory_space=pltpu.VMEM)],
        out_specs=pl.BlockSpec(memory_space=pltpu.VMEM),
        out_shape=jax.ShapeDtypeStruct((row_count, c_here, d_here), jnp.bfloat16),
        compiler_params=pltpu.CompilerParams(vmem_limit_bytes=8 << 20),
        cost_estimate=pl.CostEstimate(flops=1 << 24, bytes_accessed=amplitudes.size * 2, transcendentals=0),
    )(jnp.stack([row, col]), tile_mask, tile_irrep, amplitudes)


def expand_kernel(row_ref, irrep_ref, own_ref, other_ref, o_ref):
    row = row_ref[0]
    count = own_ref.shape[0] // BLOCK
    tiles = BLOCK // TILE
    even = row % 2 == 0
    low = lax.broadcasted_iota(jnp.int32, (BLOCK, LANES), 1) < WIN

    def at(block):
        return pl.ds(pl.multiple_of(block * BLOCK, BLOCK), BLOCK)

    def planes(i, j):
        def ordered(ref):
            value = ref[at(i ^ row), at(j ^ row)].astype(jnp.float32)
            first, second = value[:, :LANES], value[:, LANES:]
            return jnp.concatenate(
                [
                    jnp.where(low, first, pltpu.roll(second, WIN, 1)),
                    jnp.where(low, pltpu.roll(first, WIN, 1), second),
                ],
                1,
            )

        own, other = ordered(own_ref), ordered(other_ref)
        return jnp.where(even, own, other), jnp.where(even, other, own)

    def irreps(block, axis):
        tile = lax.broadcasted_iota(jnp.int32, (BLOCK, BLOCK), axis) % LANES // (TILE // 2)
        value = jnp.zeros((BLOCK, BLOCK), jnp.int32)
        for t in range(tiles):
            value = jnp.where(tile == t, irrep_ref[(block ^ row) * tiles + t], value)
        return value

    def put(plane, i, j, value):
        o_ref[plane, at(i), at(j)] = value.astype(jnp.bfloat16)

    @pl.loop(0, count)
    def _(i):
        same = irreps(i, 0) == irreps(i, 1)
        a, b = planes(i, i)
        put(0, i, i, jnp.where(same, a, 0.0))
        put(1, i, i, jnp.where(same, b, 0.0))
        put(2, i, i, jnp.where(same, 0.0, a + b.T))

        @pl.loop(i + 1, count)
        def _(j):
            same = irreps(i, 0) == irreps(j, 1)
            a_up, b_up = planes(i, j)
            a_down, b_down = planes(j, i)
            b_turned = b_down.T
            put(0, i, j, jnp.where(same, a_up + a_down.T, 0.0))
            put(1, i, j, jnp.where(same, b_up + b_turned, 0.0))
            put(2, i, j, jnp.where(same, 0.0, a_up + b_turned))
            same = irreps(j, 0) == irreps(i, 1)
            put(2, j, i, jnp.where(same, 0.0, a_down + b_up.T))


def expand(own, other, tile_irrep, row):
    vmem = pl.BlockSpec(memory_space=pltpu.VMEM)
    return pl.pallas_call(
        expand_kernel,
        in_specs=[pl.BlockSpec(memory_space=pltpu.SMEM)] * 2 + [vmem] * 2,
        out_specs=vmem,
        out_shape=jax.ShapeDtypeStruct((3, *own.shape), own.dtype),
        compiler_params=pltpu.CompilerParams(vmem_limit_bytes=6 << 20),
        cost_estimate=pl.CostEstimate(flops=1 << 24, bytes_accessed=own.size * 10, transcendentals=0),
    )(row[None], tile_irrep, own, other)


def expand_small(own, other, tile_irrep, row, row_count):
    size = own.shape[0]
    c_here = size // row_count
    even = row % 2 == 0

    def by_row(plane):
        moved = relative(plane.reshape(row_count, c_here, size), row).reshape(size // BLOCK, BLOCK, size)
        return jnp.einsum(
            "xc,jcd->jxd", deinterleave(BLOCK, True), moved, preferred_element_type=jnp.float32
        ).reshape(size, size)

    def ordered(plane):
        return by_row(by_row(plane).astype(plane.dtype).T).T

    own, other = ordered(own), ordered(other)
    a, b = jnp.where(even, own, other), jnp.where(even, other, own)
    irrep = relative(tile_irrep.reshape(row_count, c_here // TILE), row)
    order = jnp.broadcast_to(
        irrep.reshape(-1, 1, BLOCK // TILE, 1), (size // BLOCK, 2, BLOCK // TILE, TILE // 2)
    ).reshape(size)
    same = order[:, None] == order[None, :]
    block = jnp.arange(size, dtype=jnp.int32) // BLOCK
    above, level = block[:, None] < block[None, :], block[:, None] == block[None, :]

    def upper(plane):
        chosen = jnp.where(level, plane, jnp.where(above, plane + plane.T, 0.0))
        return jnp.where(same, chosen, 0.0)

    return jnp.stack([upper(a), upper(b), jnp.where(same, 0.0, a + b.T)]).astype(jnp.bfloat16)


def amplitude_planes(amplitudes, tile_mask, tile_irrep, row, col, row_count, col_count):
    _, c_here, d_here = amplitudes.shape
    to_send = pack(amplitudes, tile_mask, tile_irrep, row, col, row_count)
    mine = lax.all_to_all(to_send, "row", 0, 0)
    own = ring_gather(mine.reshape(c_here * row_count, d_here), "col", col_count)
    other = lax.ppermute(own, "row", [(i, i ^ 1) for i in range(row_count)])
    if fits(c_here, d_here):
        return expand(own, other, tile_irrep, row)
    return expand_small(own, other, tile_irrep, row, row_count)


def per_device(amplitudes, factors, tile_mask, tile_irrep, *, row_count, col_count):
    pair_count = amplitudes.shape[0]
    row, col = lax.axis_index("row"), lax.axis_index("col")
    acc = jnp.zeros((3 * WIN, LANES), jnp.float32)
    chunks = []
    start = 0
    for count in chunk_sizes(factors.shape[0] // row_count):
        pieces = {}
        for steps in (range(row_count - 1, 1, -1), range(1, -1, -1)):
            pieces.update(zip(steps, split_chunk(factors, row, start, count, row_count, list(steps))))
        arrived = [pieces[0]]
        for x in range(1, row_count):
            arrived.append(lax.ppermute(pieces[x], "row", [(i, i ^ x) for i in range(row_count)]))
        chunks.append(arrived)
        start += count
    planes = amplitude_planes(amplitudes, tile_mask, tile_irrep, row, col, row_count, col_count)
    for chunk in chunks:
        acc = contract(acc, chunk, planes)
    upper = (acc[:, :WIN] + acc[:, WIN:]).reshape(3, WIN, WIN)
    turned = upper.transpose(0, 2, 1)
    flipped = jnp.stack([upper[0] + turned[0], turned[2], upper[2], upper[1] + turned[1]])
    a_count, b_count = WIN // row_count, WIN // col_count
    blocks = flipped.reshape(pair_count, col_count, b_count, row_count, a_count).transpose(3, 1, 0, 2, 4)
    blocks = blocks.reshape(row_count * col_count, pair_count * b_count * a_count)
    summed = lax.all_to_all(blocks, ("row", "col"), 0, 0, tiled=True).sum(0)
    return summed.reshape(pair_count, b_count, a_count).transpose(0, 2, 1)


def solution(mesh):
    row_count, col_count = mesh.shape["row"], mesh.shape["col"]
    return jax.shard_map(
        functools.partial(per_device, row_count=row_count, col_count=col_count),
        mesh=mesh,
        in_specs=(P(None, "row", "col"), P("col", "row"), P(), P()),
        out_specs=P(None, "row", "col"),
        check_vma=False,
    )
```
